1024 devices in a mesh: row: 128 (over z, x, core), col: 8 (over y).
Axes of the slice: x: 8, y: 8, z: 8, core: 2. Of those that a mesh axis runs over, the one named last changes fastest.
Arguments:
- deposit_maps: float32 [16384, 8192], P('row', 'col'), may hold values from -30 to 30, as said below
- test_matrix: float32 [8192, 256], P('col'), may hold values from -1 to 1
Outputs:
- scaled_basis: float32 [16384, 256], P('row')
- projected: float32 [256, 8192], P('row', 'col')
The draws below stay inside these ranges and needn't reach their ends.
Inputs may be any that keep to these rules, and one draw needn't show every extreme that they name: `deposit_maps`: a dense real matrix.
All inputs are finite; a program needn't handle non-finite values.
Results may differ from the reference program's by a relative error of at most 0.0003.
Values sent between devices are 32-bit elements; how exact they have to be, the bound alone decides.
No kernel may reach another device: no remote copies, remote signals or barrier semaphores. Data moves between devices by JAX's collectives and lax.ppermute only.
A program may use at most 32 MiB of HBM per device.

```python
import math
import jax
import jax.numpy as jnp
from jax import lax

N = 8192
K = 256
ROWS = 16384


def draw_deposit_maps(key, part):
    subkeys = jax.random.split(jax.random.fold_in(key, 7), 7)
    ramp_values = jnp.arange(ROWS, dtype=jnp.float32) / (ROWS - 1)
    entries = jnp.clip(jax.random.normal(subkeys[0], (ROWS, N), jnp.float32), -5.0, 5.0)
    row_scale = 10.0 ** (0.5 * ramp_values + 0.5 * jax.random.uniform(subkeys[1], (ROWS,), jnp.float32))
    column_scale = 10.0 ** jax.random.uniform(subkeys[2], (N,), jnp.float32)
    floor_part = entries * column_scale[None, :]
    spread = jnp.sqrt(jnp.mean(floor_part * floor_part))
    rank_count = K // 2
    fraction = (1.0 - math.sqrt(K / N)) * (1.0 - math.sqrt(K / ROWS))
    top_amplitude = 300.0 * fraction / math.sqrt(K) * spread
    decay_steps = jnp.arange(rank_count, dtype=jnp.float32) / (rank_count - 1)
    amplitudes = top_amplitude * 10.0 ** (-2.5 * decay_steps)
    left_factor = jnp.clip(jax.random.normal(subkeys[5], (ROWS, rank_count), jnp.float32), -6.0, 6.0)
    right_factor = jnp.clip(jax.random.normal(subkeys[6], (rank_count, N), jnp.float32), -6.0, 6.0)
    structured = jnp.dot(left_factor * amplitudes[None, :], right_factor, preferred_element_type=jnp.float32, precision=lax.Precision.HIGHEST)
    normalizer = 1.0 / (top_amplitude * math.sqrt(ROWS))
    total = (floor_part + structured) * row_scale[:, None] * normalizer
    return jnp.clip(total, -30.0, 30.0)


def draw_test_matrix(key, part):
    subkey = jax.random.fold_in(key, 11)
    entries = jnp.clip(jax.random.normal(subkey, (N, K), jnp.float32), -5.0, 5.0)
    return entries / math.sqrt(N)


def setup_inputs(seed: int = 0) -> dict:
    seeds = jax.random.split(jax.random.key(seed), 3)
    deposit_maps = draw_deposit_maps(jax.random.fold_in(seeds[2], 71), 0)
    test_matrix = draw_test_matrix(jax.random.fold_in(seeds[2], 71), 0)
    return {"deposit_maps": deposit_maps, "test_matrix": test_matrix}


def apply_factor(current, gram_matrix):
    lower_factor = jnp.linalg.cholesky(gram_matrix)
    identity = jnp.eye(gram_matrix.shape[0], dtype=jnp.float32)
    inverse = jax.scipy.linalg.solve_triangular(lower_factor, identity, lower=True)
    return jnp.dot(current.astype(jnp.float32), inverse.T.astype(jnp.float32), preferred_element_type=jnp.float32, precision=lax.Precision.HIGHEST)

def reference(deposit_maps, test_matrix):
    sketch = jnp.dot(deposit_maps.astype(jnp.float32), test_matrix.astype(jnp.float32), preferred_element_type=jnp.float32, precision=lax.Precision.HIGHEST)
    current = sketch
    for sweep_index in range(2):
        gram_matrix = jnp.dot(current.T.astype(jnp.float32), current.astype(jnp.float32), preferred_element_type=jnp.float32, precision=lax.Precision.HIGHEST)
        current = apply_factor(current, gram_matrix)
    scaled_basis = current * math.sqrt(ROWS)
    projected = jnp.dot(current.T.astype(jnp.float32), deposit_maps.astype(jnp.float32), preferred_element_type=jnp.float32, precision=lax.Precision.HIGHEST)
    return (scaled_basis, projected)
```

```python
import math

import jax
import jax.numpy as jnp
from jax import lax
from jax.experimental import pallas as pl
from jax.experimental.pallas import tpu as pltpu
from jax.sharding import Mesh
from jax.sharding import PartitionSpec as P

HIGHEST = lax.Precision.HIGHEST

def invert_small(block):
    lanes = 128
    size = block.shape[0]
    entry = [[jnp.broadcast_to(block[i:i+1, j:j+1], (8, lanes)) for j in range(i + 1)] for i in range(size)]
    recip = []
    lower = [[None] * size for _ in range(size)]
    for j in range(size):
        r = lax.rsqrt(entry[j][j])
        recip.append(r)
        for i in range(j + 1, size):
            lower[i][j] = entry[i][j] * r
        for i in range(j + 1, size):
            for m in range(j + 1, i + 1):
                entry[i][m] = entry[i][m] - lower[i][j] * lower[m][j]
    inv = [[None] * size for _ in range(size)]
    for j in range(size):
        inv[j][j] = recip[j]
        for i in range(j + 1, size):
            total = lower[i][j] * inv[j][j]
            for m in range(j + 1, i):
                total = total + lower[i][m] * inv[m][j]
            inv[i][j] = -(recip[i] * total)
    return inv

def wide(x, width):
    return jnp.concatenate([x] * (width // 128), axis=1)

def factor_kernel(g_ref, w_ref, m_ref):
    n = 256
    width = 384
    row = lax.broadcasted_iota(jnp.int32, (n, n), 0)
    col = lax.broadcasted_iota(jnp.int32, (n, n), 1)
    m_ref[:, :n] = g_ref[...]
    m_ref[:, n:] = jnp.where(row == col, 1.0, 0.0).astype(jnp.float32)
    sub = lax.broadcasted_iota(jnp.int32, (8, 128), 0)
    zero = jnp.zeros((8, 128), jnp.float32)
    for half in range(2):
        base = 128 * half
        cols = slice(base, base + width)
        for p in range(16):
            k = base + 8 * p
            rows = m_ref[k:k+8, cols]
            inv = invert_small(rows[:, 8*p:8*p+8])
            panel = None
            for j in range(8):
                coef = zero
                for i in range(j, 8):
                    coef = jnp.where(sub == i, inv[i][j], coef)
                term = wide(coef, width) * jnp.broadcast_to(rows[j:j+1, :], (8, width))
                panel = term if panel is None else panel + term
            m_ref[k:k+8, cols] = panel
            if p == 15:
                continue
            solved = None
            for j in range(8):
                coef = zero
                for m in range(j + 1):
                    coef = jnp.where(sub == m, inv[j][m], coef)
                term = wide(coef, width) * jnp.broadcast_to(panel[j:j+1, :], (8, width))
                solved = term if solved is None else solved + term
            spread = [jnp.broadcast_to(solved[m:m+1, :], (8, width)) for m in range(8)]
            for rb in range(p + 1, 16):
                i = base + 8 * rb
                left = m_ref[i:i+8, k:k+8]
                acc = m_ref[i:i+8, cols]
                for m in range(8):
                    acc = acc - wide(jnp.broadcast_to(left[:, m:m+1], (8, 128)), width) * spread[m]
                m_ref[i:i+8, cols] = acc
        if half == 0:
            top = m_ref[0:128, 128:384]
            left = m_ref[0:128, 128:256].T
            m_ref[128:256, 128:384] = m_ref[128:256, 128:384] - jnp.dot(
                left, top, preferred_element_type=jnp.float32, precision=lax.Precision.HIGHEST)
    w_ref[...] = m_ref[:, n:]


def factor(gram_matrix):
    return pl.pallas_call(
        factor_kernel,
        out_shape=jax.ShapeDtypeStruct((256, 256), jnp.float32),
        in_specs=[pl.BlockSpec(memory_space=pltpu.VMEM)],
        out_specs=pl.BlockSpec(memory_space=pltpu.VMEM),
        scratch_shapes=[pltpu.VMEM((256, 512), jnp.float32)],
        name="factor",
    )(gram_matrix)


def dot(left, right, contract):
    return lax.dot_general(
        left, right, ((contract[:1], contract[1:]), ((), ())), precision=HIGHEST, preferred_element_type=jnp.float32
    )


def scatter_sum(parts, axes):
    return jnp.sum(lax.all_to_all(parts, axes, 0, 0, tiled=True), axis=0)


def spread(part, axes, count):
    return lax.all_to_all(jnp.broadcast_to(part[None], (count, *part.shape)), axes, 0, 0, tiled=True)


def sum_rows(gram_matrix):
    other = lax.ppermute(gram_matrix, "core", [(0, 1), (1, 0)])
    chip_sum = gram_matrix + other
    part = scatter_sum(chip_sum.reshape(64, 8, 128), ("z", "x"))
    return spread(part, ("z", "x"), 64).reshape(256, 256)


def on_device(deposit_maps, test_matrix):
    partial_sketch = dot(deposit_maps, test_matrix, (1, 0))
    part = scatter_sum(partial_sketch.reshape(8, 16, 256), "col")
    current = spread(part, "col", 8).reshape(128, 256)
    for sweep_index in range(2):
        inverse = factor(sum_rows(dot(current, current, (0, 0))))
        current = dot(current, inverse, (1, 1))
    total_rows = current.shape[0] * 128
    scaled_basis = current * math.sqrt(total_rows)
    projected = dot(current, deposit_maps, (0, 0))
    projected = scatter_sum(projected.reshape(128, 2, 1024), ("z", "x", "core"))
    return (scaled_basis, projected)


def solution(mesh):
    chips = Mesh(mesh.devices.reshape(8, 8, 2, 8), ("z", "x", "core", "col"))
    rows = ("z", "x", "core")
    return jax.shard_map(
        on_device,
        mesh=chips,
        in_specs=(P(rows, "col"), P("col", None)),
        out_specs=(P(rows, None), P(rows, "col")),
        check_vma=False,
    )
```

```python
import math

import jax
import jax.numpy as jnp
from jax import lax
from jax.experimental import pallas as pl
from jax.experimental.pallas import tpu as pltpu
from jax.sharding import Mesh
from jax.sharding import PartitionSpec as P

HIGHEST = lax.Precision.HIGHEST
SPLIT = 98304.0


def invert_small(block):
    size = block.shape[0]
    entry = [[jnp.broadcast_to(block[i : i + 1, j : j + 1], (8, 128)) for j in range(i + 1)] for i in range(size)]
    recip = []
    lower = [[None] * size for _ in range(size)]
    for j in range(size):
        r = lax.rsqrt(entry[j][j])
        recip.append(r)
        for i in range(j + 1, size):
            lower[i][j] = entry[i][j] * r
        for i in range(j + 1, size):
            for m in range(j + 1, i + 1):
                entry[i][m] = entry[i][m] - lower[i][j] * lower[m][j]
    inv = [[None] * size for _ in range(size)]
    for j in range(size):
        inv[j][j] = recip[j]
        for i in range(j + 1, size):
            total = lower[i][j] * inv[j][j]
            for m in range(j + 1, i):
                total = total + lower[i][m] * inv[m][j]
            inv[i][j] = -(recip[i] * total)
    return inv


def wide(x, width):
    return jnp.concatenate([x] * (width // 128), axis=1)


def eliminate(m_ref):
    width = 384
    sub = lax.broadcasted_iota(jnp.int32, (8, 128), 0)
    zero = jnp.zeros((8, 128), jnp.float32)
    for half in range(2):
        base = 128 * half
        cols = slice(base, base + width)
        for p in range(16):
            k = base + 8 * p
            rows = m_ref[k : k + 8, cols]
            inv = invert_small(rows[:, 8 * p : 8 * p + 8])
            panel = None
            for j in range(8):
                coef = zero
                for i in range(j, 8):
                    coef = jnp.where(sub == i, inv[i][j], coef)
                term = wide(coef, width) * jnp.broadcast_to(rows[j : j + 1, :], (8, width))
                panel = term if panel is None else panel + term
            m_ref[k : k + 8, cols] = panel
            if p == 15:
                continue
            solved = None
            for j in range(8):
                coef = zero
                for m in range(j + 1):
                    coef = jnp.where(sub == m, inv[j][m], coef)
                term = wide(coef, width) * jnp.broadcast_to(panel[j : j + 1, :], (8, width))
                solved = term if solved is None else solved + term
            spread_rows = [jnp.broadcast_to(solved[m : m + 1, :], (8, width)) for m in range(8)]
            for rb in range(p + 1, 16):
                i = base + 8 * rb
                left = m_ref[i : i + 8, k : k + 8]
                acc = m_ref[i : i + 8, cols]
                for m in range(8):
                    acc = acc - wide(jnp.broadcast_to(left[:, m : m + 1], (8, 128)), width) * spread_rows[m]
                m_ref[i : i + 8, cols] = acc
        if half == 0:
            top = m_ref[0:128, 128:384]
            left = m_ref[0:128, 128:256].T
            m_ref[128:256, 128:384] = m_ref[128:256, 128:384] - jnp.dot(
                left, top, preferred_element_type=jnp.float32, precision=HIGHEST
            )


def two_sum(a, b):
    t = a + b
    z = t - a
    return t, (a - (t - z)) + (b - z)


def add_pairs(a_hi, a_lo, b_hi, b_lo):
    hi, err = two_sum(a_hi, b_hi)
    return hi, err + (a_lo + b_lo)


def slices_of(x, bound, count, tail=None):
    out = []
    for a in range(count):
        step = bound * (SPLIT * 2.0 ** (-8 * a))
        part = (x + step) - step
        x = x - part
        out.append(part)
        if tail is not None and a == 2:
            x = x + tail
    return out


def sum_products(lefts, rights, contract):
    order = sorted((a + b, a, b) for a in range(len(lefts)) for b in range(len(rights)))
    hi = lo = None
    for rank, a, b in order:
        prod = lax.dot_general(lefts[a], rights[b], (contract, ((), ())), preferred_element_type=jnp.float32)
        if hi is None:
            hi, lo = prod, jnp.zeros_like(prod)
        elif rank <= 2:
            hi, err = two_sum(hi, prod)
            lo = lo + err
        else:
            lo = lo + prod
    return two_sum(hi, lo)


def gram_kernel(s_ref, o_ref):
    x = s_ref[...]
    bound = jnp.max(jnp.abs(x), axis=0, keepdims=True)
    parts = slices_of(x, bound, 3)
    rights = [part.astype(jnp.bfloat16) for part in parts]
    lefts = [part.T.astype(jnp.bfloat16) for part in parts]
    for c in range(2):
        pair = sum_products([left[128 * c : 128 * c + 128] for left in lefts], rights, ((1,), (0,)))
        for rb in range(16):
            for h in range(2):
                for w in range(2):
                    o_ref[32 * c + 2 * rb + h, w] = pair[w][8 * rb : 8 * rb + 8, 128 * h : 128 * h + 128]


def chip_kernel(a_ref, b_ref, o_ref):
    o_ref[:, 0], o_ref[:, 1] = add_pairs(a_ref[:, 0], a_ref[:, 1], b_ref[:, 0], b_ref[:, 1])


def total_kernel(a_ref, o_ref):
    pairs = [(a_ref[i, 0], a_ref[i, 1]) for i in range(64)]
    while len(pairs) > 1:
        pairs = [add_pairs(*pairs[i], *pairs[i + 1]) for i in range(0, len(pairs), 2)]
    hi, lo = two_sum(*pairs[0])
    for i in range(64):
        o_ref[i, 0] = hi
        o_ref[i, 1] = lo


def power_below(x):
    return ((x + x * 8.429369702178807e-08) - x) * 8388608.0


def factor_kernel(v_ref, w_ref, m_ref, hi_ref, lo_ref, g_ref, f_ref, t_ref):
    n = 256
    for rb in range(32):
        for h in range(2):
            hi_ref[8 * rb : 8 * rb + 8, 128 * h : 128 * h + 128] = v_ref[2 * rb + h, 0]
            lo_ref[8 * rb : 8 * rb + 8, 128 * h : 128 * h + 128] = v_ref[2 * rb + h, 1]
    diagonal = lax.broadcasted_iota(jnp.int32, (n, n), 0) == lax.broadcasted_iota(jnp.int32, (n, n), 1)
    identity = jnp.where(diagonal, 1.0, 0.0).astype(jnp.float32)
    on_diagonal = jnp.where(diagonal, hi_ref[...], 0.0)
    scale_row = power_below(lax.rsqrt(jnp.sum(on_diagonal, axis=0, keepdims=True)))
    scale_col = power_below(lax.rsqrt(jnp.sum(on_diagonal, axis=1, keepdims=True)))
    hi = hi_ref[...] * scale_row * scale_col
    lo = lo_ref[...] * scale_row * scale_col
    for a, part in enumerate(slices_of(hi, 1.0, 5, lo)):
        g_ref[a] = part.astype(jnp.bfloat16)
    m_ref[:, :n] = hi
    m_ref[:, n:] = identity
    eliminate(m_ref)
    first = m_ref[:, n:]
    parts = slices_of(first, jnp.max(jnp.abs(first), axis=1, keepdims=True), 3)
    for a, part in enumerate(parts):
        f_ref[a] = part.astype(jnp.bfloat16)
    hi_ref[...] = parts[0] + (parts[1] + parts[2])
    for c in range(2):
        rows = slice(128 * c, 128 * c + 128)
        hi, lo = sum_products([f_ref[a, rows] for a in range(3)], [g_ref[a] for a in range(5)], ((1,), (0,)))
        for a, part in enumerate(slices_of(hi, 1.0, 5, lo)):
            t_ref[a, rows] = part.astype(jnp.bfloat16)
    for c in range(2):
        rows = slice(128 * c, 128 * c + 128)
        hi, lo = sum_products([t_ref[a, rows] for a in range(5)], [f_ref[a] for a in range(3)], ((1,), (1,)))
        m_ref[rows, :n] = hi
    m_ref[:, n:] = identity
    eliminate(m_ref)
    w_ref[...] = scale_row * jnp.dot(
        m_ref[:, n:], hi_ref[...], preferred_element_type=jnp.float32, precision=HIGHEST
    )


def call(kernel, shape, *args, scratch=()):
    vmem = pl.BlockSpec(memory_space=pltpu.VMEM)
    return pl.pallas_call(
        kernel,
        out_shape=jax.ShapeDtypeStruct(shape, jnp.float32),
        in_specs=[vmem] * len(args),
        out_specs=vmem,
        scratch_shapes=scratch,
        name=kernel.__name__,
    )(*args)


PAIRS = (64, 2, 8, 128)


def inverse_factor(pairs):
    return call(
        factor_kernel,
        (256, 256),
        pairs,
        scratch=[
            pltpu.VMEM((256, 512), jnp.float32),
            pltpu.VMEM((256, 256), jnp.float32),
            pltpu.VMEM((256, 256), jnp.float32),
            pltpu.VMEM((5, 256, 256), jnp.bfloat16),
            pltpu.VMEM((3, 256, 256), jnp.bfloat16),
            pltpu.VMEM((5, 256, 256), jnp.bfloat16),
        ],
    )


def dot(left, right, contract):
    return lax.dot_general(
        left, right, ((contract[:1], contract[1:]), ((), ())), precision=HIGHEST, preferred_element_type=jnp.float32
    )


def exchange(parts, axes):
    return lax.all_to_all(parts, axes, 0, 0, tiled=True)


def scatter_sum(parts, axes):
    return jnp.sum(exchange(parts, axes), axis=0)


def spread(part, axes, count):
    return exchange(jnp.broadcast_to(part[None], (count, *part.shape)), axes)


def on_device(deposit_maps, test_matrix):
    partial_sketch = dot(deposit_maps, test_matrix, (1, 0))
    part = scatter_sum(partial_sketch.reshape(8, 16, 256), "col")
    sketch = spread(part, "col", 8).reshape(128, 256)
    mine = call(gram_kernel, PAIRS, sketch)
    other = lax.ppermute(mine, "core", [(0, 1), (1, 0)])
    chip = call(chip_kernel, PAIRS, mine, other)
    total = call(total_kernel, PAIRS, exchange(chip, ("z", "x")))
    inverse = inverse_factor(exchange(total, ("z", "x")))
    orthonormal = dot(sketch, inverse, (1, 1))
    total_rows = orthonormal.shape[0] * 128
    scaled_basis = orthonormal * math.sqrt(total_rows)
    halves = dot(orthonormal, deposit_maps, (0, 0)).reshape(64, 2, 2, 1024).transpose(1, 0, 2, 3)
    projected = scatter_sum(scatter_sum(halves, "core"), ("z", "x"))
    return (scaled_basis, projected)


def solution(mesh):
    chips = Mesh(mesh.devices.reshape(8, 8, 2, 8), ("z", "x", "core", "col"))
    rows = ("z", "x", "core")
    return jax.shard_map(
        on_device,
        mesh=chips,
        in_specs=(P(rows, "col"), P("col", None)),
        out_specs=(P(rows, None), P(rows, "col")),
        check_vma=False,
    )
```

```python
import math

import jax
import jax.numpy as jnp
from jax import lax
from jax.experimental import pallas as pl
from jax.experimental.pallas import tpu as pltpu
from jax.sharding import Mesh
from jax.sharding import PartitionSpec as P

HIGHEST = lax.Precision.HIGHEST
SPLIT = 98304.0


def invert_small(block):
    size = block.shape[0]
    entry = [[jnp.broadcast_to(block[i : i + 1, j : j + 1], (8, 128)) for j in range(i + 1)] for i in range(size)]
    recip = []
    lower = [[None] * size for _ in range(size)]
    for j in range(size):
        r = lax.rsqrt(entry[j][j])
        recip.append(r)
        for i in range(j + 1, size):
            lower[i][j] = entry[i][j] * r
        for i in range(j + 1, size):
            for m in range(j + 1, i + 1):
                entry[i][m] = entry[i][m] - lower[i][j] * lower[m][j]
    inv = [[None] * size for _ in range(size)]
    for j in range(size):
        inv[j][j] = recip[j]
        for i in range(j + 1, size):
            total = lower[i][j] * inv[j][j]
            for m in range(j + 1, i):
                total = total + lower[i][m] * inv[m][j]
            inv[i][j] = -(recip[i] * total)
    return inv


def wide(x, width):
    return jnp.concatenate([x] * (width // 128), axis=1)


def eliminate(m_ref):
    width = 384
    sub = lax.broadcasted_iota(jnp.int32, (8, 128), 0)
    zero = jnp.zeros((8, 128), jnp.float32)
    for half in range(2):
        base = 128 * half
        cols = slice(base, base + width)
        for p in range(16):
            k = base + 8 * p
            rows = m_ref[k : k + 8, cols]
            inv = invert_small(rows[:, 8 * p : 8 * p + 8])
            panel = None
            for j in range(8):
                coef = zero
                for i in range(j, 8):
                    coef = jnp.where(sub == i, inv[i][j], coef)
                term = wide(coef, width) * jnp.broadcast_to(rows[j : j + 1, :], (8, width))
                panel = term if panel is None else panel + term
            m_ref[k : k + 8, cols] = panel
            if p == 15:
                continue
            solved = None
            for j in range(8):
                coef = zero
                for m in range(j + 1):
                    coef = jnp.where(sub == m, inv[j][m], coef)
                term = wide(coef, width) * jnp.broadcast_to(panel[j : j + 1, :], (8, width))
                solved = term if solved is None else solved + term
            spread_rows = [jnp.broadcast_to(solved[m : m + 1, :], (8, width)) for m in range(8)]
            for rb in range(p + 1, 16):
                i = base + 8 * rb
                left = m_ref[i : i + 8, k : k + 8]
                acc = m_ref[i : i + 8, cols]
                for m in range(8):
                    acc = acc - wide(jnp.broadcast_to(left[:, m : m + 1], (8, 128)), width) * spread_rows[m]
                m_ref[i : i + 8, cols] = acc
        if half == 0:
            top = m_ref[0:128, 128:384]
            left = m_ref[0:128, 128:256].T
            m_ref[128:256, 128:384] = m_ref[128:256, 128:384] - jnp.dot(
                left, top, preferred_element_type=jnp.float32, precision=HIGHEST
            )


def two_sum(a, b):
    t = a + b
    z = t - a
    return t, (a - (t - z)) + (b - z)


def top_half(shape):
    return lax.broadcasted_iota(jnp.int32, shape, len(shape) - 2) % 8 < 4


def swap(x):
    return pltpu.roll(x, 4, x.ndim - 2)


def slices_of(x, bound, count, tail=None):
    out = []
    for a in range(count):
        step = bound * (SPLIT * 2.0 ** (-8 * a))
        part = (x + step) - step
        x = x - part
        out.append(part)
        if tail is not None and a == 2:
            x = x + tail
    return out


def sum_products(lefts, rights, contract, last_rank=8):
    order = sorted((a + b, a, b) for a in range(len(lefts)) for b in range(len(rights)))
    hi = lo = None
    for rank, a, b in order:
        if rank > last_rank:
            break
        prod = lax.dot_general(lefts[a], rights[b], (contract, ((), ())), preferred_element_type=jnp.float32)
        if hi is None:
            hi, lo = prod, jnp.zeros_like(prod)
        elif rank <= 2:
            hi, err = two_sum(hi, prod)
            lo = lo + err
        else:
            lo = lo + prod
    return two_sum(hi, lo)


def gram_kernel(s_ref, o_ref):
    x = s_ref[...]
    bound = jnp.max(jnp.abs(x), axis=0, keepdims=True)
    parts = slices_of(x, bound, 3)
    rights = [part.astype(jnp.bfloat16) for part in parts]
    lefts = [part.T.astype(jnp.bfloat16) for part in parts]
    for c in range(2):
        hi, lo = sum_products([left[128 * c : 128 * c + 128] for left in lefts], rights, ((1,), (0,)))
        for tile in range(32):
            block = (slice(8 * (tile // 2), 8 * (tile // 2) + 8), slice(128 * (tile % 2), 128 * (tile % 2) + 128))
            o_ref[c, 2 * tile] = jnp.where(top_half((8, 128)), hi[block], swap(lo[block]))
            o_ref[c, 2 * tile + 1] = jnp.where(top_half((8, 128)), swap(hi[block]), lo[block])


def chip_kernel(a_ref, o_ref):
    total, err = two_sum(a_ref[0], a_ref[1])
    o_ref[...] = total + jnp.where(top_half(err.shape), 0.0, swap(err))


def total_kernel(a_ref, o_ref):
    terms = [(a_ref[i], None) for i in range(64)]
    while len(terms) > 1:
        merged = []
        for (x, x_err), (y, y_err) in zip(terms[::2], terms[1::2]):
            total, err = two_sum(x, y)
            merged.append((total, err if x_err is None else err + (x_err + y_err)))
        terms = merged
    total, err = terms[0]
    total = total + jnp.where(top_half((8, 128)), 0.0, swap(err))
    for i in range(64):
        o_ref[i] = total


def power_below(x):
    return ((x + x * 8.429369702178807e-08) - x) * 8388608.0


def factor_kernel(core_ref, mine_ref, other_ref, w_ref, m_ref, hi_ref, lo_ref, g_ref, f_ref, t_ref):
    n = 256
    for half_ref, base in ((mine_ref, 128 * core_ref[0]), (other_ref, 128 * (1 - core_ref[0]))):
        for tile in range(32):
            first, second = half_ref[2 * tile], half_ref[2 * tile + 1]
            rows = pl.ds(pl.multiple_of(base + 8 * (tile // 2), 8), 8)
            cols = slice(128 * (tile % 2), 128 * (tile % 2) + 128)
            hi, lo = two_sum(
                jnp.where(top_half((8, 128)), first, swap(second)), jnp.where(top_half((8, 128)), swap(first), second)
            )
            hi_ref[rows, cols] = hi
            lo_ref[rows, cols] = lo
    diagonal = lax.broadcasted_iota(jnp.int32, (n, n), 0) == lax.broadcasted_iota(jnp.int32, (n, n), 1)
    identity = jnp.where(diagonal, 1.0, 0.0).astype(jnp.float32)
    on_diagonal = jnp.where(diagonal, hi_ref[...], 0.0)
    scale_row = power_below(lax.rsqrt(jnp.sum(on_diagonal, axis=0, keepdims=True)))
    scale_col = power_below(lax.rsqrt(jnp.sum(on_diagonal, axis=1, keepdims=True)))
    hi = hi_ref[...] * scale_row * scale_col
    lo = lo_ref[...] * scale_row * scale_col
    for a, part in enumerate(slices_of(hi, 1.0, 5, lo)):
        g_ref[a] = part.astype(jnp.bfloat16)
    m_ref[:, :n] = hi
    m_ref[:, n:] = identity
    eliminate(m_ref)
    first = m_ref[:, n:]
    parts = slices_of(first, jnp.max(jnp.abs(first), axis=1, keepdims=True), 3)
    for a, part in enumerate(parts):
        f_ref[a] = part.astype(jnp.bfloat16)
    hi_ref[...] = parts[0] + (parts[1] + parts[2])
    for c in range(2):
        rows = slice(128 * c, 128 * c + 128)
        hi, lo = sum_products([f_ref[a, rows] for a in range(3)], [g_ref[a] for a in range(5)], ((1,), (0,)))
        for a, part in enumerate(slices_of(hi, 1.0, 5, lo)):
            t_ref[a, rows] = part.astype(jnp.bfloat16)
    for c in range(2):
        rows = slice(128 * c, 128 * c + 128)
        hi, lo = sum_products([t_ref[a, rows] for a in range(5)], [f_ref[a] for a in range(3)], ((1,), (1,)), 4)
        m_ref[rows, :n] = hi
    m_ref[:, n:] = identity
    eliminate(m_ref)
    w_ref[...] = scale_row * jnp.dot(
        m_ref[:, n:], hi_ref[...], preferred_element_type=jnp.float32, precision=HIGHEST
    )


def call(kernel, shape, *args, scalar=None, scratch=()):
    vmem = pl.BlockSpec(memory_space=pltpu.VMEM)
    specs = [vmem] * len(args)
    if scalar is not None:
        args = (scalar, *args)
        specs = [pl.BlockSpec(memory_space=pltpu.SMEM), *specs]
    return pl.pallas_call(
        kernel,
        out_shape=jax.ShapeDtypeStruct(shape, jnp.float32),
        in_specs=specs,
        out_specs=vmem,
        scratch_shapes=scratch,
        name=kernel.__name__,
    )(*args)


HALF = (64, 8, 128)


def inverse_factor(core, mine, other):
    return call(
        factor_kernel,
        (256, 256),
        mine,
        other,
        scalar=core,
        scratch=[
            pltpu.VMEM((256, 512), jnp.float32),
            pltpu.VMEM((256, 256), jnp.float32),
            pltpu.VMEM((256, 256), jnp.float32),
            pltpu.VMEM((5, 256, 256), jnp.bfloat16),
            pltpu.VMEM((3, 256, 256), jnp.bfloat16),
            pltpu.VMEM((5, 256, 256), jnp.bfloat16),
        ],
    )


def dot(left, right, contract):
    return lax.dot_general(
        left, right, ((contract[:1], contract[1:]), ((), ())), precision=HIGHEST, preferred_element_type=jnp.float32
    )


def exchange(parts, axes):
    return lax.all_to_all(parts, axes, 0, 0, tiled=True)


def scatter_sum(parts, axes):
    return jnp.sum(exchange(parts, axes), axis=0)


def spread(part, axes, count):
    return exchange(jnp.broadcast_to(part[None], (count, *part.shape)), axes)


def on_device(deposit_maps, test_matrix):
    partial_sketch = dot(deposit_maps, test_matrix, (1, 0))
    part = scatter_sum(partial_sketch.reshape(8, 16, 256), "col")
    sketch = spread(part, "col", 8).reshape(128, 256)
    pairs = exchange(call(gram_kernel, (2, *HALF), sketch), "core")
    chip = call(chip_kernel, HALF, pairs)
    mine = exchange(call(total_kernel, HALF, exchange(chip, ("z", "x"))), ("z", "x"))
    other = lax.ppermute(mine, "core", [(0, 1), (1, 0)])
    inverse = inverse_factor(lax.axis_index("core").reshape(1), mine, other)
    orthonormal = dot(sketch, inverse, (1, 1))
    total_rows = orthonormal.shape[0] * 128
    scaled_basis = orthonormal * math.sqrt(total_rows)
    halves = dot(orthonormal, deposit_maps, (0, 0)).reshape(64, 2, 2, 1024).transpose(1, 0, 2, 3)
    projected = scatter_sum(scatter_sum(halves, "core"), ("z", "x"))
    return (scaled_basis, projected)


def solution(mesh):
    chips = Mesh(mesh.devices.reshape(8, 8, 2, 8), ("z", "x", "core", "col"))
    rows = ("z", "x", "core")
    return jax.shard_map(
        on_device,
        mesh=chips,
        in_specs=(P(rows, "col"), P("col", None)),
        out_specs=(P(rows, None), P(rows, "col")),
        check_vma=False,
    )
```

```python
import math

import jax
import jax.numpy as jnp
from jax import lax
from jax.experimental import pallas as pl
from jax.experimental.pallas import tpu as pltpu
from jax.sharding import Mesh
from jax.sharding import PartitionSpec as P

HIGHEST = lax.Precision.HIGHEST
SPLIT = 98304.0


def invert_small(block):
    size = block.shape[0]
    entry = [[jnp.broadcast_to(block[i : i + 1, j : j + 1], (8, 128)) for j in range(i + 1)] for i in range(size)]
    recip = []
    lower = [[None] * size for _ in range(size)]
    for j in range(size):
        r = lax.rsqrt(entry[j][j])
        recip.append(r)
        for i in range(j + 1, size):
            lower[i][j] = entry[i][j] * r
        for i in range(j + 1, size):
            for m in range(j + 1, i + 1):
                entry[i][m] = entry[i][m] - lower[i][j] * lower[m][j]
    inv = [[None] * size for _ in range(size)]
    for j in range(size):
        inv[j][j] = recip[j]
        for i in range(j + 1, size):
            total = lower[i][j] * inv[j][j]
            for m in range(j + 1, i):
                total = total + lower[i][m] * inv[m][j]
            inv[i][j] = -(recip[i] * total)
    return inv


def wide(x, width):
    return jnp.concatenate([x] * (width // 128), axis=1)


def eliminate(m_ref):
    width = 384
    sub = lax.broadcasted_iota(jnp.int32, (8, 128), 0)
    zero = jnp.zeros((8, 128), jnp.float32)
    for half in range(2):
        base = 128 * half
        cols = slice(base, base + width)
        for p in range(16):
            k = base + 8 * p
            rows = m_ref[k : k + 8, cols]
            inv = invert_small(rows[:, 8 * p : 8 * p + 8])
            panel = None
            for j in range(8):
                coef = zero
                for i in range(j, 8):
                    coef = jnp.where(sub == i, inv[i][j], coef)
                term = wide(coef, width) * jnp.broadcast_to(rows[j : j + 1, :], (8, width))
                panel = term if panel is None else panel + term
            m_ref[k : k + 8, cols] = panel
            if p == 15:
                continue
            solved = None
            for j in range(8):
                coef = zero
                for m in range(j + 1):
                    coef = jnp.where(sub == m, inv[j][m], coef)
                term = wide(coef, width) * jnp.broadcast_to(panel[j : j + 1, :], (8, width))
                solved = term if solved is None else solved + term
            spread_rows = [jnp.broadcast_to(solved[m : m + 1, :], (8, width)) for m in range(8)]
            for rb in range(p + 1, 16):
                i = base + 8 * rb
                left = m_ref[i : i + 8, k : k + 8]
                acc = m_ref[i : i + 8, cols]
                for m in range(8):
                    acc = acc - wide(jnp.broadcast_to(left[:, m : m + 1], (8, 128)), width) * spread_rows[m]
                m_ref[i : i + 8, cols] = acc
        if half == 0:
            top = m_ref[0:128, 128:384]
            left = m_ref[0:128, 128:256].T
            m_ref[128:256, 128:384] = m_ref[128:256, 128:384] - jnp.dot(
                left, top, preferred_element_type=jnp.float32, precision=HIGHEST
            )


def two_sum(a, b):
    t = a + b
    z = t - a
    return t, (a - (t - z)) + (b - z)


def top_half(shape):
    return lax.broadcasted_iota(jnp.int32, shape, len(shape) - 2) % 8 < 4


def swap(x):
    return pltpu.roll(x, 4, x.ndim - 2)


def slices_of(x, bound, count, tail=None):
    out = []
    for a in range(count):
        step = bound * (SPLIT * 2.0 ** (-8 * a))
        part = (x + step) - step
        x = x - part
        out.append(part)
        if tail is not None and a == 2:
            x = x + tail
    return out


def sum_products(lefts, rights, contract, last_rank=8):
    order = sorted((a + b, a, b) for a in range(len(lefts)) for b in range(len(rights)))
    hi = lo = None
    for rank, a, b in order:
        if rank > last_rank:
            break
        prod = lax.dot_general(lefts[a], rights[b], (contract, ((), ())), preferred_element_type=jnp.float32)
        if hi is None:
            hi, lo = prod, jnp.zeros_like(prod)
        elif rank <= 2:
            hi, err = two_sum(hi, prod)
            lo = lo + err
        else:
            lo = lo + prod
    return two_sum(hi, lo)


def gram_kernel(core_ref, s_ref, o_ref):
    mine = pl.ds(pl.multiple_of(128 * core_ref[0], 128), 128)
    sides = []
    for x in (s_ref[:, mine], s_ref[...]):
        sides.append(slices_of(x, jnp.max(jnp.abs(x), axis=0, keepdims=True), 3))
    lefts = [part.T.astype(jnp.bfloat16) for part in sides[0]]
    rights = [part.astype(jnp.bfloat16) for part in sides[1]]
    hi, lo = sum_products(lefts, rights, ((1,), (0,)))
    for tile in range(32):
        block = (slice(8 * (tile // 2), 8 * (tile // 2) + 8), slice(128 * (tile % 2), 128 * (tile % 2) + 128))
        o_ref[2 * tile] = jnp.where(top_half((8, 128)), hi[block], swap(lo[block]))
        o_ref[2 * tile + 1] = jnp.where(top_half((8, 128)), swap(hi[block]), lo[block])


def total_kernel(a_ref, o_ref):
    terms = [(a_ref[i], None) for i in range(64)]
    while len(terms) > 1:
        merged = []
        for (x, x_err), (y, y_err) in zip(terms[::2], terms[1::2]):
            total, err = two_sum(x, y)
            merged.append((total, err if x_err is None else err + (x_err + y_err)))
        terms = merged
    total, err = terms[0]
    total = total + jnp.where(top_half((8, 128)), 0.0, swap(err))
    for i in range(64):
        o_ref[i] = total


def power_below(x):
    return ((x + x * 8.429369702178807e-08) - x) * 8388608.0


def factor_kernel(core_ref, mine_ref, other_ref, w_ref, m_ref, hi_ref, lo_ref, g_ref, f_ref, t_ref):
    n = 256
    for half_ref, base in ((mine_ref, 128 * core_ref[0]), (other_ref, 128 * (1 - core_ref[0]))):
        for tile in range(32):
            first, second = half_ref[2 * tile], half_ref[2 * tile + 1]
            rows = pl.ds(pl.multiple_of(base + 8 * (tile // 2), 8), 8)
            cols = slice(128 * (tile % 2), 128 * (tile % 2) + 128)
            hi, lo = two_sum(
                jnp.where(top_half((8, 128)), first, swap(second)), jnp.where(top_half((8, 128)), swap(first), second)
            )
            hi_ref[rows, cols] = hi
            lo_ref[rows, cols] = lo
    diagonal = lax.broadcasted_iota(jnp.int32, (n, n), 0) == lax.broadcasted_iota(jnp.int32, (n, n), 1)
    identity = jnp.where(diagonal, 1.0, 0.0).astype(jnp.float32)
    on_diagonal = jnp.where(diagonal, hi_ref[...], 0.0)
    scale_row = power_below(lax.rsqrt(jnp.sum(on_diagonal, axis=0, keepdims=True)))
    scale_col = power_below(lax.rsqrt(jnp.sum(on_diagonal, axis=1, keepdims=True)))
    hi = hi_ref[...] * scale_row * scale_col
    lo = lo_ref[...] * scale_row * scale_col
    for a, part in enumerate(slices_of(hi, 1.0, 5, lo)):
        g_ref[a] = part.astype(jnp.bfloat16)
    m_ref[:, :n] = hi
    m_ref[:, n:] = identity
    eliminate(m_ref)
    first = m_ref[:, n:]
    parts = slices_of(first, jnp.max(jnp.abs(first), axis=1, keepdims=True), 3)
    for a, part in enumerate(parts):
        f_ref[a] = part.astype(jnp.bfloat16)
    hi_ref[...] = parts[0] + (parts[1] + parts[2])
    for c in range(2):
        rows = slice(128 * c, 128 * c + 128)
        hi, lo = sum_products([f_ref[a, rows] for a in range(3)], [g_ref[a] for a in range(5)], ((1,), (0,)))
        for a, part in enumerate(slices_of(hi, 1.0, 5, lo)):
            t_ref[a, rows] = part.astype(jnp.bfloat16)
    for c in range(2):
        rows = slice(128 * c, 128 * c + 128)
        hi, lo = sum_products([t_ref[a, rows] for a in range(5)], [f_ref[a] for a in range(3)], ((1,), (1,)), 4)
        m_ref[rows, :n] = hi
    m_ref[:, n:] = identity
    eliminate(m_ref)
    w_ref[...] = scale_row * jnp.dot(
        m_ref[:, n:], hi_ref[...], preferred_element_type=jnp.float32, precision=HIGHEST
    )


def call(kernel, shape, *args, scalar=None, scratch=()):
    vmem = pl.BlockSpec(memory_space=pltpu.VMEM)
    specs = [vmem] * len(args)
    if scalar is not None:
        args = (scalar, *args)
        specs = [pl.BlockSpec(memory_space=pltpu.SMEM), *specs]
    return pl.pallas_call(
        kernel,
        out_shape=jax.ShapeDtypeStruct(shape, jnp.float32),
        in_specs=specs,
        out_specs=vmem,
        scratch_shapes=scratch,
        name=kernel.__name__,
    )(*args)


HALF = (64, 8, 128)


def inverse_factor(core, mine, other):
    return call(
        factor_kernel,
        (256, 256),
        mine,
        other,
        scalar=core,
        scratch=[
            pltpu.VMEM((256, 512), jnp.float32),
            pltpu.VMEM((256, 256), jnp.float32),
            pltpu.VMEM((256, 256), jnp.float32),
            pltpu.VMEM((5, 256, 256), jnp.bfloat16),
            pltpu.VMEM((3, 256, 256), jnp.bfloat16),
            pltpu.VMEM((5, 256, 256), jnp.bfloat16),
        ],
    )


def dot(left, right, contract):
    return lax.dot_general(
        left, right, ((contract[:1], contract[1:]), ((), ())), precision=HIGHEST, preferred_element_type=jnp.float32
    )


def exchange(parts, axes):
    return lax.all_to_all(parts, axes, 0, 0, tiled=True)


def scatter_sum(parts, axes):
    return jnp.sum(exchange(parts, axes), axis=0)


def spread(part, axes, count):
    return exchange(jnp.broadcast_to(part[None], (count, *part.shape)), axes)


def on_device(deposit_maps, test_matrix):
    partial_sketch = dot(deposit_maps, test_matrix, (1, 0))
    part = scatter_sum(partial_sketch.reshape(8, 16, 256), "col")
    core = lax.axis_index("core").reshape(1)
    chip = spread(part, ("core", "col"), 16).reshape(256, 256)
    sketch = lax.dynamic_slice_in_dim(chip, 128 * core[0], 128)
    pairs = call(gram_kernel, HALF, chip, scalar=core)
    mine = exchange(call(total_kernel, HALF, exchange(pairs, ("z", "x"))), ("z", "x"))
    other = lax.ppermute(mine, "core", [(0, 1), (1, 0)])
    inverse = inverse_factor(core, mine, other)
    orthonormal = dot(sketch, inverse, (1, 1))
    total_rows = orthonormal.shape[0] * 128
    scaled_basis = orthonormal * math.sqrt(total_rows)
    halves = dot(orthonormal, deposit_maps, (0, 0)).reshape(64, 2, 2, 1024).transpose(1, 0, 2, 3)
    projected = scatter_sum(scatter_sum(halves, "core"), ("z", "x"))
    return (scaled_basis, projected)


def solution(mesh):
    chips = Mesh(mesh.devices.reshape(8, 8, 2, 8), ("z", "x", "core", "col"))
    rows = ("z", "x", "core")
    return jax.shard_map(
        on_device,
        mesh=chips,
        in_specs=(P(rows, "col"), P("col", None)),
        out_specs=(P(rows, None), P(rows, "col")),
        check_vma=False,
    )
```
